32 devices in a mesh: samples: 4 (over y, x), channel: 4 (over z), spatial: 2 (over core).
Axes of the slice: x: 2, y: 2, z: 4, core: 2. Of those that a mesh axis runs over, the one named last changes fastest.
Arguments:
- features: bfloat16 [512, 4, 2, 1024], P('channel', 'samples', 'spatial'), may hold values from -6 to 6
- conv_one: bfloat16 [27, 512, 512], P(None, 'channel'), may hold values from -0.0625 to 0.0625
- conv_two: bfloat16 [27, 512, 512], P(None, 'channel'), may hold values from -0.0625 to 0.0625
- cotangent: bfloat16 [512, 4, 2, 1024], P('channel', 'samples', 'spatial'), may hold values from -6 to 6
Outputs:
- mixed_out: bfloat16 [512, 4, 2, 1024], P('channel', 'samples', 'spatial')
- input_grad: bfloat16 [512, 4, 2, 1024], P('channel', 'samples', 'spatial')
- grad_one: float32 [27, 512, 512], P(None, 'channel')
- grad_two: float32 [27, 512, 512], P(None, 'channel')
The draws below stay inside these ranges and needn't reach their ends.
All inputs are finite; a program needn't handle non-finite values.
Results may differ from the reference program's by a relative error of at most 0.017.
Values may be sent and summed in bfloat16 or wider, within the bound.
A program may use at most 128 MiB of HBM per device.

```python
import jax
import jax.numpy as jnp
from jax import lax

C = 512
SIDE = 32
CROPS = 4
DEPTH = 2
PLANE = 1024


def spiked(values, key, source, target, blocks, factor):
    owner, partner = [(jnp.arange(values.shape[position]) // (values.shape[position] // blocks)).reshape([-1 if axis == position else 1 for axis in range(values.ndim)]) for position in (source, target)]
    chosen = jax.random.permutation(key, blocks)[partner]
    strong = (owner == chosen) | (owner == (partner + blocks // 2) % blocks)
    return jnp.where(strong, factor * values, values)


def level_of(stream_key, dims, split, low, top_value):
    level = 1.0
    for position, shards_of in split:
        draws = jax.random.uniform(jax.random.fold_in(jax.random.fold_in(stream_key, 6), position), (shards_of,), jnp.float32, low / len(split), top_value / len(split))
        level = level * jnp.repeat(jnp.exp(draws), dims[position] // shards_of).reshape((-1,) + (1,) * (len(dims) - 1 - position))
    return level


def scatter_about(own_key, shape, deviation, limit, shards=(), held_as=jnp.bfloat16):
    loudness = level_of(own_key, shape, shards, -0.22, 0.18) if shards else 1.0
    values = jax.random.normal(own_key, shape, jnp.float32) * deviation * loudness
    return jnp.minimum(jnp.maximum(values, -limit), limit).astype(held_as)


def noise_with(stream_key, extent, spread, limit, split, heavy, held_as=jnp.bfloat16):
    drawn = spread * jax.random.normal(stream_key, extent, jnp.float32)
    if split:
        drawn = drawn * level_of(stream_key, extent, split, -0.22, 0.18)
    return jnp.clip(spiked(drawn, jax.random.fold_in(stream_key, 3), *heavy), -limit, limit).astype(held_as)


def setup_inputs(seed: int = 0) -> dict:
    streams_of = jax.random.split(jax.random.key(seed), 5)
    features = scatter_about(streams_of[0], (C, CROPS, DEPTH, PLANE), 1.0, 6.0, ((0, 4), (1, 4), (2, 2)))
    conv_one = noise_with(streams_of[1], (27, C, C), (27 * C) ** -0.5, 0.0625, ((1, 4),), (1, 2, 4, 2.0))
    conv_two = noise_with(streams_of[2], (27, C, C), (27 * C) ** -0.5, 0.0625, ((1, 4),), (1, 2, 4, 2.0))
    cotangent = scatter_about(streams_of[3], (C, CROPS, DEPTH, PLANE), 1.0, 6.0, ((0, 4), (1, 4), (2, 2)))
    return {"features": features, "conv_one": conv_one, "conv_two": conv_two, "cotangent": cotangent}


def to_grid(values):
    return values.reshape(values.shape[0], values.shape[1], values.shape[2], SIDE, SIDE)

def to_flat(values):
    return values.reshape(values.shape[0], values.shape[1], values.shape[2], SIDE * SIDE)

def as_taps(kernel):
    return kernel.reshape(3, 3, 3, kernel.shape[1], kernel.shape[2])

def forward_conv(source, kernel, rhs_spec, depth_pad):
    return lax.conv_general_dilated(source, as_taps(kernel), (1, 1, 1), [(depth_pad, depth_pad), (1, 1), (1, 1)], dimension_numbers=('CNDHW', rhs_spec, 'CNDHW'), preferred_element_type=jnp.float32)

def data_grad(source, kernel, rhs_spec, depth_pad):
    flipped = as_taps(kernel)[::-1, ::-1, ::-1]
    return lax.conv_general_dilated(source, flipped, (1, 1, 1), [(depth_pad, depth_pad), (1, 1), (1, 1)], dimension_numbers=('CNDHW', rhs_spec, 'CNDHW'), preferred_element_type=jnp.float32)

def weight_grad(padded, upstream, out_spec):
    result = lax.conv_general_dilated(padded, upstream, (1, 1, 1), [(0, 0), (0, 0), (0, 0)], dimension_numbers=('NCDHW', 'OIDHW', out_spec), preferred_element_type=jnp.float32)
    return result.reshape(27, result.shape[3], result.shape[4])

def reference(features, conv_one, conv_two, cotangent):
    source = to_grid(features)
    upstream = to_grid(cotangent)
    pre_act = forward_conv(source, conv_one, 'DHWOI', 1)
    hidden = jax.nn.silu(pre_act).astype(jnp.bfloat16)
    mixed_out = forward_conv(hidden, conv_two, 'DHWIO', 1).astype(jnp.bfloat16)
    hidden_grad = data_grad(upstream, conv_two, 'DHWOI', 1)
    sigmoid_v = jax.nn.sigmoid(pre_act)
    act_grad = (hidden_grad * sigmoid_v * (1.0 + pre_act * (1.0 - sigmoid_v))).astype(jnp.bfloat16)
    input_grad = data_grad(act_grad, conv_one, 'DHWIO', 1).astype(jnp.bfloat16)
    widths = ((0, 0), (0, 0), (1, 1), (1, 1), (1, 1))
    grad_two = weight_grad(jnp.pad(hidden, widths), upstream, 'DHWNC')
    grad_one = weight_grad(jnp.pad(source, widths), act_grad, 'DHWCN')
    return (to_flat(mixed_out), to_flat(input_grad), grad_one, grad_two)
```

```python
import functools
import math

import jax
import jax.numpy as jnp
from jax import lax
from jax.experimental import pallas as pl
from jax.experimental.pallas import tpu as pltpu
from jax.sharding import PartitionSpec as P

LANES = 256
ROWS = 16


def shifted(values, dy, dx, side):
    plane = values.shape[1]
    amount = (-(dy * side + dx)) % plane
    if amount == 0:
        return values
    cell = lax.broadcasted_iota(jnp.int32, values.shape, 1)
    row, col = cell // side + dy, cell % side + dx
    inside = (row >= 0) & (row < side) & (col >= 0) & (col < side)
    return jnp.where(inside, pltpu.roll(values, amount, 1), 0.0)


def offsets(sign):
    return [(sign * (b - 1), sign * (c - 1)) for b in range(3) for c in range(3)]


def other_tap(sign):
    s = lax.axis_index("spatial")
    return 2 - 2 * s if sign > 0 else 2 * s


def product_over_channels(sign, side, own_ref, oth_ref, w_ref, y_ref, finish):
    held = w_ref.shape[0] // 27
    plane = own_ref.shape[1]
    third = 9 * held
    away = pl.multiple_of(other_tap(sign) * third, third)

    @pl.loop(0, plane // LANES)
    def _(n):
        cols = pl.ds(pl.multiple_of(n * LANES, LANES), LANES)
        y_ref[:, cols] = jnp.dot(
            w_ref[third : 2 * third, :], own_ref[:, cols], preferred_element_type=jnp.float32
        ) + jnp.dot(
            w_ref[pl.ds(away, third), :], oth_ref[:, cols], preferred_element_type=jnp.float32
        )

    @pl.loop(0, held // ROWS)
    def _(k):
        base = pl.multiple_of(k * ROWS, ROWS)
        total = None
        for t, (dy, dx) in enumerate(offsets(sign)):
            part = shifted(y_ref[pl.ds(base + t * held, ROWS), :], dy, dx, side)
            total = part if total is None else total + part
        finish(pl.ds(base, ROWS), total)


def forward_kernel(side, own_ref, oth_ref, w_ref, pre_ref, hid_ref, y_ref):
    def finish(rows, total):
        pre_ref[rows, :] = total
        hid_ref[rows, :] = (total / (1.0 + jnp.exp(-total))).astype(jnp.bfloat16)

    product_over_channels(1, side, own_ref, oth_ref, w_ref, y_ref, finish)


def backward_kernel(side, own_ref, oth_ref, w_ref, pre_ref, act_ref, y_ref):
    def finish(rows, total):
        pre = pre_ref[rows, :]
        sig = 1.0 / (1.0 + jnp.exp(-pre))
        act_ref[rows, :] = (total * sig * (1.0 + pre * (1.0 - sig))).astype(jnp.bfloat16)

    product_over_channels(-1, side, own_ref, oth_ref, w_ref, y_ref, finish)


NT = (((1,), (1,)), ((), ()))
TN = (((0,), (0,)), ((), ()))


def weight_kernel(sign, side, own_ref, oth_ref, far_own_ref, far_oth_ref, cols_ref, grad_ref):
    held = own_ref.shape[0]
    third = 9 * held
    half = third // 2

    @pl.loop(0, held // ROWS)
    def _(k):
        base = pl.multiple_of(k * ROWS, ROWS)
        for j, ref in enumerate((own_ref, oth_ref)):
            values = ref[pl.ds(base, ROWS), :].astype(jnp.float32)
            for t, (dy, dx) in enumerate(offsets(sign)):
                cols_ref[pl.ds(base + (j * 9 + t) * held, ROWS), :] = shifted(values, dy, dx, side).astype(jnp.bfloat16)

    mine = pl.multiple_of(lax.axis_index("spatial") * half, half)

    @pl.loop(0, far_own_ref.shape[0] // LANES)
    def _(n):
        rows = pl.ds(pl.multiple_of(n * LANES, LANES), LANES)
        far_own, far_oth = far_own_ref[rows, :], far_oth_ref[rows, :]
        grad_ref[:third, rows] = lax.dot_general(
            cols_ref[third:, :], far_own, NT, preferred_element_type=jnp.float32
        ).astype(jnp.bfloat16)
        grad_ref[third:, rows] = (
            lax.dot_general(cols_ref[pl.ds(mine, half), :], far_own, NT, preferred_element_type=jnp.float32)
            + lax.dot_general(cols_ref[pl.ds(third + mine, half), :], far_oth, NT, preferred_element_type=jnp.float32)
        ).astype(jnp.bfloat16)


def mix_kernel(sign, cols_ref, w_ref, out_ref):
    third = w_ref.shape[0] // 3
    away = pl.multiple_of(other_tap(sign) * third, third)

    @pl.loop(0, out_ref.shape[0] // LANES)
    def _(n):
        rows = pl.ds(pl.multiple_of(n * LANES, LANES), LANES)
        out_ref[rows, :] = (
            lax.dot_general(w_ref[third : 2 * third, rows], cols_ref[:third, :], TN, preferred_element_type=jnp.float32)
            + lax.dot_general(w_ref[pl.ds(away, third), rows], cols_ref[third:, :], TN, preferred_element_type=jnp.float32)
        ).astype(jnp.bfloat16)


def call(kernel, outs, scratch, flops, moved, *args):
    vmem = pl.BlockSpec(memory_space=pltpu.VMEM)
    return pl.pallas_call(
        kernel,
        out_shape=outs,
        in_specs=[vmem] * len(args),
        out_specs=jax.tree.map(lambda _: vmem, outs),
        scratch_shapes=scratch,
        cost_estimate=pl.CostEstimate(flops=flops, bytes_accessed=moved, transcendentals=0),
        compiler_params=pltpu.CompilerParams(vmem_limit_bytes=32 * 1024 * 1024),
    )(*args)


def swap(values):
    return lax.ppermute(values, "spatial", [(0, 1), (1, 0)])


def total_over_samples(part):
    return lax.psum(part, "samples")


def joined(mine, theirs, sign, held):
    third = 9 * held
    first = lax.axis_index("spatial") == 0
    zero = jnp.where(first, mine, theirs)
    one = jnp.where(first, theirs, mine)
    low, high = (one, zero) if sign > 0 else (zero, one)
    whole = jnp.concatenate([low[:third], zero[third:], one[third:], high[:third]], axis=0)
    return whole.astype(jnp.float32).reshape(27, held, whole.shape[1])


def body(features, conv_one, conv_two, cotangent):
    held, plane = features.shape[0], features.shape[3]
    full = conv_one.shape[2]
    side = math.isqrt(plane)
    third = 9 * held
    f32, b16 = jnp.float32, jnp.bfloat16
    flat = lambda v: v.reshape(held, plane)
    w_one, w_two = conv_one.reshape(27 * held, full), conv_two.reshape(27 * held, full)
    gather = lambda v: lax.all_gather(v, "channel", axis=0, tiled=True)
    work = 2 * 2 * third * full * plane
    small = 6 * held * full

    x = gather(flat(features))
    c = gather(flat(cotangent))
    x_oth, c_oth = swap(x), swap(c)
    y_scratch = [pltpu.VMEM((third, plane), f32)]
    pre, hid = call(
        functools.partial(forward_kernel, side),
        (jax.ShapeDtypeStruct((held, plane), f32), jax.ShapeDtypeStruct((held, plane), b16)),
        y_scratch, work, small, x, x_oth, w_one,
    )
    hid_oth = swap(hid)
    act = call(
        functools.partial(backward_kernel, side),
        jax.ShapeDtypeStruct((held, plane), b16),
        y_scratch, work, small, c, c_oth, w_two, pre,
    )
    act_oth = swap(act)
    grads = lambda sign, own, oth, far, far_oth: call(
        functools.partial(weight_kernel, sign, side),
        (jax.ShapeDtypeStruct((2 * third, plane), b16), jax.ShapeDtypeStruct((third + third // 2, full), b16)),
        [], work, small, own, oth, far, far_oth,
    )
    mix = lambda sign, cols, w: call(
        functools.partial(mix_kernel, sign),
        jax.ShapeDtypeStruct((full, plane), b16),
        [], work, small, cols, w,
    )
    scatter = lambda v: lax.psum_scatter(v, "channel", scatter_dimension=0, tiled=True)
    cols_h, part_two = grads(1, hid, hid_oth, c, c_oth)
    sum_two = total_over_samples(part_two)
    cols_g, part_one = grads(-1, act, act_oth, x, x_oth)
    sum_one = total_over_samples(part_one)
    mixed = scatter(mix(1, cols_h, w_two)).reshape(features.shape)
    input_grad = scatter(mix(-1, cols_g, w_one)).reshape(features.shape)
    grad_two = joined(sum_two, swap(sum_two), 1, held)
    grad_one = joined(sum_one, swap(sum_one), -1, held)
    return mixed, input_grad, grad_one, grad_two


def solution(mesh):
    act = P("channel", "samples", "spatial", None)
    ker = P(None, "channel", None)
    return jax.shard_map(
        body,
        mesh=mesh,
        in_specs=(act, ker, ker, act),
        out_specs=(act, act, ker, ker),
        check_vma=False,
    )
```

```python
import functools
import math

import jax
import jax.numpy as jnp
from jax import lax
from jax.experimental import pallas as pl
from jax.experimental.pallas import tpu as pltpu
from jax.sharding import PartitionSpec as P

LANES = 256
ROWS = 16


def shifted(values, dy, dx, side):
    plane = values.shape[1]
    amount = (-(dy * side + dx)) % plane
    if amount == 0:
        return values
    cell = lax.broadcasted_iota(jnp.int32, values.shape, 1)
    row, col = cell // side + dy, cell % side + dx
    inside = (row >= 0) & (row < side) & (col >= 0) & (col < side)
    return jnp.where(inside, pltpu.roll(values, amount, 1), 0.0)


def offsets(sign):
    return [(sign * (b - 1), sign * (c - 1)) for b in range(3) for c in range(3)]


def other_tap(sign):
    s = lax.axis_index("spatial")
    return 2 - 2 * s if sign > 0 else 2 * s


def product_over_channels(sign, side, own_ref, oth_ref, w_ref, y_ref, finish):
    held = w_ref.shape[0] // 27
    plane = own_ref.shape[1]
    third = 9 * held
    away = pl.multiple_of(other_tap(sign) * third, third)

    @pl.loop(0, plane // LANES)
    def _(n):
        cols = pl.ds(pl.multiple_of(n * LANES, LANES), LANES)
        y_ref[:, cols] = jnp.dot(
            w_ref[third : 2 * third, :], own_ref[:, cols], preferred_element_type=jnp.float32
        ) + jnp.dot(
            w_ref[pl.ds(away, third), :], oth_ref[:, cols], preferred_element_type=jnp.float32
        )

    @pl.loop(0, held // ROWS)
    def _(k):
        base = pl.multiple_of(k * ROWS, ROWS)
        total = None
        for t, (dy, dx) in enumerate(offsets(sign)):
            part = shifted(y_ref[pl.ds(base + t * held, ROWS), :], dy, dx, side)
            total = part if total is None else total + part
        finish(pl.ds(base, ROWS), total)


def forward_kernel(side, own_ref, oth_ref, w_ref, pre_ref, hid_ref, y_ref):
    def finish(rows, total):
        pre_ref[rows, :] = total
        hid_ref[rows, :] = (total / (1.0 + jnp.exp(-total))).astype(jnp.bfloat16)

    product_over_channels(1, side, own_ref, oth_ref, w_ref, y_ref, finish)


def backward_kernel(side, own_ref, oth_ref, w_ref, pre_ref, act_ref, y_ref):
    def finish(rows, total):
        pre = pre_ref[rows, :]
        sig = 1.0 / (1.0 + jnp.exp(-pre))
        act_ref[rows, :] = (total * sig * (1.0 + pre * (1.0 - sig))).astype(jnp.bfloat16)

    product_over_channels(-1, side, own_ref, oth_ref, w_ref, y_ref, finish)


NT = (((1,), (1,)), ((), ()))
TN = (((0,), (0,)), ((), ()))


def weight_kernel(sign, side, own_ref, oth_ref, far_own_ref, far_oth_ref, cols_ref, grad_ref):
    held = own_ref.shape[0]
    third = 9 * held
    half = third // 2

    @pl.loop(0, held // ROWS)
    def _(k):
        base = pl.multiple_of(k * ROWS, ROWS)
        for j, ref in enumerate((own_ref, oth_ref)):
            values = ref[pl.ds(base, ROWS), :].astype(jnp.float32)
            for t, (dy, dx) in enumerate(offsets(sign)):
                cols_ref[pl.ds(base + (j * 9 + t) * held, ROWS), :] = shifted(values, dy, dx, side).astype(jnp.bfloat16)

    mine = pl.multiple_of(lax.axis_index("spatial") * half, half)

    @pl.loop(0, far_own_ref.shape[0] // LANES)
    def _(n):
        rows = pl.ds(pl.multiple_of(n * LANES, LANES), LANES)
        far_own, far_oth = far_own_ref[rows, :], far_oth_ref[rows, :]
        grad_ref[:third, rows] = lax.dot_general(
            cols_ref[third:, :], far_own, NT, preferred_element_type=jnp.float32
        ).astype(jnp.bfloat16)
        grad_ref[third:, rows] = (
            lax.dot_general(cols_ref[pl.ds(mine, half), :], far_own, NT, preferred_element_type=jnp.float32)
            + lax.dot_general(cols_ref[pl.ds(third + mine, half), :], far_oth, NT, preferred_element_type=jnp.float32)
        ).astype(jnp.bfloat16)


def mix_kernel(sign, cols_ref, w_ref, out_ref):
    third = w_ref.shape[0] // 3
    away = pl.multiple_of(other_tap(sign) * third, third)

    @pl.loop(0, out_ref.shape[0] // LANES)
    def _(n):
        rows = pl.ds(pl.multiple_of(n * LANES, LANES), LANES)
        out_ref[rows, :] = (
            lax.dot_general(w_ref[third : 2 * third, rows], cols_ref[:third, :], TN, preferred_element_type=jnp.float32)
            + lax.dot_general(w_ref[pl.ds(away, third), rows], cols_ref[third:, :], TN, preferred_element_type=jnp.float32)
        ).astype(jnp.bfloat16)


def call(kernel, outs, scratch, flops, moved, *args):
    vmem = pl.BlockSpec(memory_space=pltpu.VMEM)
    return pl.pallas_call(
        kernel,
        out_shape=outs,
        in_specs=[vmem] * len(args),
        out_specs=jax.tree.map(lambda _: vmem, outs),
        scratch_shapes=scratch,
        cost_estimate=pl.CostEstimate(flops=flops, bytes_accessed=moved, transcendentals=0),
        compiler_params=pltpu.CompilerParams(vmem_limit_bytes=32 * 1024 * 1024),
    )(*args)


def swap(values):
    return lax.ppermute(values, "spatial", [(0, 1), (1, 0)])


def shift(values, axis, by):
    n = lax.axis_size(axis)
    return lax.ppermute(values, axis, [(i, (i + by) % n) for i in range(n)])


def gathered(values):
    n, rows = lax.axis_size("channel"), values.shape[0]
    if n > 4:
        return lax.all_gather(values, "channel", axis=0, tiled=True)
    me = lax.axis_index("channel")
    whole = jnp.zeros((n * rows,) + values.shape[1:], values.dtype)
    for k in range(n):
        piece = values if k == 0 else shift(values, "channel", k)
        whole = lax.dynamic_update_slice(whole, piece, (((me - k) % n) * rows, 0))
    return whole


def scattered(values):
    n = lax.axis_size("channel")
    if n > 4:
        return lax.psum_scatter(values, "channel", scatter_dimension=0, tiled=True)
    me, rows = lax.axis_index("channel"), values.shape[0] // n
    total = 0.0
    for k in range(n):
        piece = lax.dynamic_slice(values, (((me + k) % n) * rows, 0), (rows, values.shape[1]))
        piece = piece if k == 0 else shift(piece, "channel", k)
        total = total + piece.astype(jnp.float32)
    return total.astype(values.dtype)


def halved_and_joined(values, bits):
    n, me = lax.axis_size("samples"), lax.axis_index("samples")
    trade = lambda v, bit: lax.ppermute(v, "samples", [(i, i ^ bit) for i in range(n)])
    rows = values.shape[0]
    for bit in bits:
        high = (me // bit) % 2
        cols = values.shape[1] // 2
        cut = lambda at: lax.dynamic_slice(values, (0, at * cols), (rows, cols))
        kept, sent = cut(high), cut(1 - high)
        got = trade(sent, bit)
        values = (kept.astype(jnp.float32) + got.astype(jnp.float32)).astype(values.dtype)
    for bit in bits[::-1]:
        high = (me // bit) % 2
        got = trade(values, bit)
        values = jnp.concatenate([jnp.where(high == 0, values, got), jnp.where(high == 0, got, values)], axis=1)
    return values


def total_over_samples(part):
    if lax.axis_size("samples") != 4 or part.shape[1] % 512 or part.shape[0] % 16:
        return lax.psum(part, "samples")
    middle = part.shape[0] // 2
    return jnp.concatenate([halved_and_joined(part[:middle], (1, 2)), halved_and_joined(part[middle:], (2, 1))], axis=0)


def joined(mine, theirs, sign, held):
    third = 9 * held
    first = lax.axis_index("spatial") == 0
    zero = jnp.where(first, mine, theirs)
    one = jnp.where(first, theirs, mine)
    low, high = (one, zero) if sign > 0 else (zero, one)
    whole = jnp.concatenate([low[:third], zero[third:], one[third:], high[:third]], axis=0)
    return whole.astype(jnp.float32).reshape(27, held, whole.shape[1])


def body(features, conv_one, conv_two, cotangent):
    held, plane = features.shape[0], features.shape[3]
    full = conv_one.shape[2]
    side = math.isqrt(plane)
    third = 9 * held
    f32, b16 = jnp.float32, jnp.bfloat16
    flat = lambda v: v.reshape(held, plane)
    w_one, w_two = conv_one.reshape(27 * held, full), conv_two.reshape(27 * held, full)
    work = 2 * 2 * third * full * plane
    small = 6 * held * full

    x = gathered(flat(features))
    c = gathered(flat(cotangent))
    x_oth, c_oth = swap(x), swap(c)
    y_scratch = [pltpu.VMEM((third, plane), f32)]
    pre, hid = call(
        functools.partial(forward_kernel, side),
        (jax.ShapeDtypeStruct((held, plane), f32), jax.ShapeDtypeStruct((held, plane), b16)),
        y_scratch, work, small, x, x_oth, w_one,
    )
    hid_oth = swap(hid)
    act = call(
        functools.partial(backward_kernel, side),
        jax.ShapeDtypeStruct((held, plane), b16),
        y_scratch, work, small, c, c_oth, w_two, pre,
    )
    act_oth = swap(act)
    grads = lambda sign, own, oth, far, far_oth: call(
        functools.partial(weight_kernel, sign, side),
        (jax.ShapeDtypeStruct((2 * third, plane), b16), jax.ShapeDtypeStruct((third + third // 2, full), b16)),
        [], work, small, own, oth, far, far_oth,
    )
    mix = lambda sign, cols, w: call(
        functools.partial(mix_kernel, sign),
        jax.ShapeDtypeStruct((full, plane), b16),
        [], work, small, cols, w,
    )
    cols_h, part_two = grads(1, hid, hid_oth, c, c_oth)
    sum_two = total_over_samples(part_two)
    cols_g, part_one = grads(-1, act, act_oth, x, x_oth)
    sum_one = total_over_samples(part_one)
    mixed = scattered(mix(1, cols_h, w_two)).reshape(features.shape)
    input_grad = scattered(mix(-1, cols_g, w_one)).reshape(features.shape)
    grad_two = joined(sum_two, swap(sum_two), 1, held)
    grad_one = joined(sum_one, swap(sum_one), -1, held)
    return mixed, input_grad, grad_one, grad_two


def solution(mesh):
    act = P("channel", "samples", "spatial", None)
    ker = P(None, "channel", None)
    return jax.shard_map(
        body,
        mesh=mesh,
        in_specs=(act, ker, ker, act),
        out_specs=(act, act, ker, ker),
        check_vma=False,
    )
```

```python
import functools
import math

import jax
import jax.numpy as jnp
from jax import lax
from jax.experimental import pallas as pl
from jax.experimental.pallas import tpu as pltpu
from jax.sharding import PartitionSpec as P


LANES = 256
ROWS = 16


def shifted(values, dy, dx, side):
    plane = values.shape[1]
    amount = (-(dy * side + dx)) % plane
    if amount == 0:
        return values
    cell = lax.broadcasted_iota(jnp.int32, values.shape, 1)
    row, col = cell // side + dy, cell % side + dx
    inside = (row >= 0) & (row < side) & (col >= 0) & (col < side)
    return jnp.where(inside, pltpu.roll(values, amount, 1), 0.0)


def offsets(sign):
    return [(sign * (b - 1), sign * (c - 1)) for b in range(3) for c in range(3)]


def other_tap(sign):
    s = lax.axis_index("spatial")
    return 2 - 2 * s if sign > 0 else 2 * s


def product_over_channels(sign, side, own_ref, oth_ref, w_ref, y_ref, finish):
    held = w_ref.shape[0] // 27
    plane = own_ref.shape[1]
    third = 9 * held
    away = pl.multiple_of(other_tap(sign) * third, third)

    @pl.loop(0, plane // LANES)
    def _(n):
        cols = pl.ds(pl.multiple_of(n * LANES, LANES), LANES)
        y_ref[:, cols] = jnp.dot(
            w_ref[third : 2 * third, :], own_ref[:, cols], preferred_element_type=jnp.float32
        ) + jnp.dot(
            w_ref[pl.ds(away, third), :], oth_ref[:, cols], preferred_element_type=jnp.float32
        )

    @pl.loop(0, held // ROWS)
    def _(k):
        base = pl.multiple_of(k * ROWS, ROWS)
        total = None
        for t, (dy, dx) in enumerate(offsets(sign)):
            part = shifted(y_ref[pl.ds(base + t * held, ROWS), :], dy, dx, side)
            total = part if total is None else total + part
        finish(pl.ds(base, ROWS), total)


def forward_kernel(side, own_ref, oth_ref, w_ref, pre_ref, hid_ref, y_ref):
    def finish(rows, total):
        pre_ref[rows, :] = total
        hid_ref[rows, :] = (total / (1.0 + jnp.exp(-total))).astype(jnp.bfloat16)

    product_over_channels(1, side, own_ref, oth_ref, w_ref, y_ref, finish)


def backward_kernel(side, own_ref, oth_ref, w_ref, pre_ref, act_ref, y_ref):
    def finish(rows, total):
        pre = pre_ref[rows, :]
        sig = 1.0 / (1.0 + jnp.exp(-pre))
        act_ref[rows, :] = (total * sig * (1.0 + pre * (1.0 - sig))).astype(jnp.bfloat16)

    product_over_channels(-1, side, own_ref, oth_ref, w_ref, y_ref, finish)


NT = (((1,), (1,)), ((), ()))
TN = (((0,), (0,)), ((), ()))


def weight_kernel(sign, side, own_ref, oth_ref, far_own_ref, far_oth_ref, w_ref, grad_ref, out_ref, cols_ref):
    held = own_ref.shape[0]
    third = 9 * held
    half = third // 2

    @pl.loop(0, held // ROWS)
    def _(k):
        base = pl.multiple_of(k * ROWS, ROWS)
        for j, ref in enumerate((own_ref, oth_ref)):
            values = ref[pl.ds(base, ROWS), :].astype(jnp.float32)
            for t, (dy, dx) in enumerate(offsets(sign)):
                cols_ref[pl.ds(base + (j * 9 + t) * held, ROWS), :] = shifted(values, dy, dx, side).astype(jnp.bfloat16)

    mine = pl.multiple_of(lax.axis_index("spatial") * half, half)
    away = pl.multiple_of(other_tap(sign) * third, third)

    @pl.loop(0, far_own_ref.shape[0] // LANES)
    def _(n):
        rows = pl.ds(pl.multiple_of(n * LANES, LANES), LANES)
        far_own, far_oth = far_own_ref[rows, :], far_oth_ref[rows, :]
        grad_ref[:third, rows] = lax.dot_general(
            cols_ref[third:, :], far_own, NT, preferred_element_type=jnp.float32
        ).astype(jnp.bfloat16)
        grad_ref[third:, rows] = (
            lax.dot_general(cols_ref[pl.ds(mine, half), :], far_own, NT, preferred_element_type=jnp.float32)
            + lax.dot_general(cols_ref[pl.ds(third + mine, half), :], far_oth, NT, preferred_element_type=jnp.float32)
        ).astype(jnp.bfloat16)
        out_ref[rows, :] = (
            lax.dot_general(w_ref[third : 2 * third, rows], cols_ref[:third, :], TN, preferred_element_type=jnp.float32)
            + lax.dot_general(w_ref[pl.ds(away, third), rows], cols_ref[third:, :], TN, preferred_element_type=jnp.float32)
        ).astype(jnp.bfloat16)


def cols_kernel(sign, side, own_ref, oth_ref, cols_ref):
    held = own_ref.shape[0]

    @pl.loop(0, held // ROWS)
    def _(k):
        base = pl.multiple_of(k * ROWS, ROWS)
        for j, ref in enumerate((own_ref, oth_ref)):
            values = ref[pl.ds(base, ROWS), :].astype(jnp.float32)
            for t, (dy, dx) in enumerate(offsets(sign)):
                cols_ref[pl.ds(base + (j * 9 + t) * held, ROWS), :] = shifted(values, dy, dx, side).astype(jnp.bfloat16)


def block_kernel(cols_ref, own_a_ref, own_b_ref, oth_a_ref, oth_b_ref, a_ref, b_ref, own_ref, oth_ref):
    held = own_a_ref.shape[0]
    third = 9 * held
    half = third // 2
    own_ref[:held, :], own_ref[held:, :] = own_a_ref[...], own_b_ref[...]
    oth_ref[:held, :], oth_ref[held:, :] = oth_a_ref[...], oth_b_ref[...]
    mine = pl.multiple_of(lax.axis_index("spatial") * half, half)
    dot = lambda rows, far: lax.dot_general(rows, far[...], NT, preferred_element_type=jnp.float32)
    away = dot(cols_ref[third:, :], own_ref).astype(jnp.bfloat16)
    a_ref[:third, :], b_ref[:third, :] = away[:, :held], away[:, held:]
    near = dot(cols_ref[pl.ds(mine, half), :], own_ref) + dot(cols_ref[pl.ds(third + mine, half), :], oth_ref)
    near = near.astype(jnp.bfloat16)
    a_ref[third:, :], b_ref[third:, :] = near[:, :held], near[:, held:]


def mix_kernel(sign, cols_ref, w_ref, out_ref):
    third = w_ref.shape[0] // 3
    away = pl.multiple_of(other_tap(sign) * third, third)

    @pl.loop(0, out_ref.shape[0] // LANES)
    def _(n):
        rows = pl.ds(pl.multiple_of(n * LANES, LANES), LANES)
        out_ref[rows, :] = (
            lax.dot_general(w_ref[third : 2 * third, rows], cols_ref[:third, :], TN, preferred_element_type=jnp.float32)
            + lax.dot_general(w_ref[pl.ds(away, third), rows], cols_ref[third:, :], TN, preferred_element_type=jnp.float32)
        ).astype(jnp.bfloat16)


def call(kernel, outs, scratch, flops, moved, *args):
    vmem = pl.BlockSpec(memory_space=pltpu.VMEM)
    return pl.pallas_call(
        kernel,
        out_shape=outs,
        in_specs=[vmem] * len(args),
        out_specs=jax.tree.map(lambda _: vmem, outs),
        scratch_shapes=scratch,
        cost_estimate=pl.CostEstimate(flops=flops, bytes_accessed=moved, transcendentals=0),
        compiler_params=pltpu.CompilerParams(vmem_limit_bytes=32 * 1024 * 1024),
    )(*args)


def swap(values):
    return lax.ppermute(values, "spatial", [(0, 1), (1, 0)])


def shift(values, axis, by):
    n = lax.axis_size(axis)
    return lax.ppermute(values, axis, [(i, (i + by) % n) for i in range(n)])


def pieces_of(values):
    pieces = [values]
    for k in range(1, lax.axis_size("channel")):
        pieces.append(shift(values, "channel", k))
    return pieces


def placed(pieces, axis):
    n, me = lax.axis_size("channel"), lax.axis_index("channel")
    shape = list(pieces[0].shape)
    size = shape[axis]
    shape[axis] = n * size
    whole = jnp.zeros(shape, pieces[0].dtype)
    for k, piece in enumerate(pieces):
        whole = lax.dynamic_update_slice_in_dim(whole, piece, ((me - k) % n) * size, axis)
    return whole


def gathered(values):
    if lax.axis_size("channel") > 4:
        return lax.all_gather(values, "channel", axis=0, tiled=True)
    return placed(pieces_of(values), 0)


def scattered(values):
    n = lax.axis_size("channel")
    if n > 4:
        return lax.psum_scatter(values, "channel", scatter_dimension=0, tiled=True)
    me, rows = lax.axis_index("channel"), values.shape[0] // n
    total = 0.0
    for k in range(n):
        piece = lax.dynamic_slice(values, (((me + k) % n) * rows, 0), (rows, values.shape[1]))
        piece = piece if k == 0 else shift(piece, "channel", k)
        total = total + piece.astype(jnp.float32)
    return total.astype(values.dtype)


def halved_and_joined(values, bits, axis):
    n, me = lax.axis_size("samples"), lax.axis_index("samples")
    trade = lambda v, bit: lax.ppermute(v, "samples", [(i, i ^ bit) for i in range(n)])
    for bit in bits:
        high = (me // bit) % 2
        size = values.shape[axis] // 2
        kept = lax.dynamic_slice_in_dim(values, high * size, size, axis)
        sent = lax.dynamic_slice_in_dim(values, (1 - high) * size, size, axis)
        got = trade(sent, bit)
        values = (kept.astype(jnp.float32) + got.astype(jnp.float32)).astype(values.dtype)
    for bit in bits[::-1]:
        high = (me // bit) % 2
        got = trade(values, bit)
        values = jnp.concatenate([jnp.where(high == 0, values, got), jnp.where(high == 0, got, values)], axis=axis)
    return values


def total_over_samples(part):
    if lax.axis_size("samples") != 4 or part.shape[1] % 512 or part.shape[0] % 16:
        return lax.psum(part, "samples")
    middle = part.shape[0] // 2
    return jnp.concatenate([halved_and_joined(part[:middle], (1, 2), 1), halved_and_joined(part[middle:], (2, 1), 1)], axis=0)


def join_kernel(sign, mine_ref, theirs_ref, out_ref):
    block = pl.program_id(0)
    half = out_ref.shape[0]
    s = lax.axis_index("spatial")
    low = 1 if sign > 0 else 0
    source = jnp.where(block < 2, low, jnp.where(block > 3, 1 - low, block - 2))
    part = jnp.where(block < 2, block, jnp.where(block > 3, block - 4, 2))
    rows = pl.ds(pl.multiple_of(part * half, half), half)

    @pl.when(source == s)
    def _():
        out_ref[...] = mine_ref[rows, :].astype(jnp.float32)

    @pl.when(source != s)
    def _():
        out_ref[...] = theirs_ref[rows, :].astype(jnp.float32)


def joined(mine, theirs, sign, held):
    half, full = 9 * held // 2, mine.shape[1]
    whole = pl.BlockSpec(memory_space=pltpu.VMEM)
    out = pl.pallas_call(
        functools.partial(join_kernel, sign),
        out_shape=jax.ShapeDtypeStruct((6 * half, full), jnp.float32),
        grid=(6,),
        in_specs=[whole, whole],
        out_specs=pl.BlockSpec((half, full), lambda j: (j, 0)),
        cost_estimate=pl.CostEstimate(flops=0, bytes_accessed=36 * half * full, transcendentals=0),
        compiler_params=pltpu.CompilerParams(vmem_limit_bytes=16 * 1024 * 1024),
    )(mine, theirs)
    return out.reshape(27, held, full)


def body(features, conv_one, conv_two, cotangent):
    held, plane = features.shape[0], features.shape[3]
    full = conv_one.shape[2]
    side = math.isqrt(plane)
    third = 9 * held
    f32, b16 = jnp.float32, jnp.bfloat16
    flat = lambda v: v.reshape(held, plane)
    w_one, w_two = conv_one.reshape(27 * held, full), conv_two.reshape(27 * held, full)
    work = 2 * 2 * third * full * plane
    small = 6 * held * full

    x = gathered(flat(features))
    x_oth = swap(x)
    small_mesh = lax.axis_size("channel") == 4 and lax.axis_size("samples") == 4 and held % 128 == 0
    if small_mesh:
        c_own = pieces_of(flat(cotangent))
        c_far = []
        for piece in c_own:
            c_far.append(swap(piece))
        c, c_oth = placed(c_own, 0), placed(c_far, 0)
    else:
        c = gathered(flat(cotangent))
        c_oth = swap(c)
    y_scratch = [pltpu.VMEM((third, plane), f32)]
    pre, hid = call(
        functools.partial(forward_kernel, side),
        (jax.ShapeDtypeStruct((held, plane), f32), jax.ShapeDtypeStruct((held, plane), b16)),
        y_scratch, work, small, x, x_oth, w_one,
    )
    hid_oth = swap(hid)
    act = call(
        functools.partial(backward_kernel, side),
        jax.ShapeDtypeStruct((held, plane), b16),
        y_scratch, work, small, c, c_oth, w_two, pre,
    )
    act_oth = swap(act)
    weights = lambda sign, own, oth, far, far_oth, w: call(
        functools.partial(weight_kernel, sign, side),
        (jax.ShapeDtypeStruct((third + third // 2, full), b16), jax.ShapeDtypeStruct((full, plane), b16)),
        [pltpu.VMEM((2 * third, plane), b16)], 2 * work, small, own, oth, far, far_oth, w,
    )
    if small_mesh:
        cols = call(
            functools.partial(cols_kernel, 1, side),
            jax.ShapeDtypeStruct((2 * third, plane), b16),
            [], held * plane, small, hid, hid_oth,
        )
        blocks = []
        for k in (0, 2):
            block = jax.ShapeDtypeStruct((third + third // 2, held), b16)
            far = pltpu.VMEM((2 * held, plane), b16)
            pair = call(
                block_kernel, (block, block), [far, far], work // 2, small,
                cols, c_own[k], c_own[k + 1], c_far[k], c_far[k + 1],
            )
            for part, bits in zip(pair, ((1, 2), (2, 1))):
                blocks.append(halved_and_joined(part, bits, 0))
        sum_two = placed(blocks, 1)
        mix_two = call(
            functools.partial(mix_kernel, 1),
            jax.ShapeDtypeStruct((full, plane), b16),
            [], work, small, cols, w_two,
        )
    else:
        part_two, mix_two = weights(1, hid, hid_oth, c, c_oth, w_two)
        sum_two = total_over_samples(part_two)
    part_one, mix_one = weights(-1, act, act_oth, x, x_oth, w_one)
    mixed = scattered(mix_two).reshape(features.shape)
    input_grad = scattered(mix_one).reshape(features.shape)
    sum_one = total_over_samples(part_one)
    grad_two = joined(sum_two, swap(sum_two), 1, held)
    grad_one = joined(sum_one, swap(sum_one), -1, held)
    return mixed, input_grad, grad_one, grad_two


def solution(mesh):
    act = P("channel", "samples", "spatial", None)
    ker = P(None, "channel", None)
    return jax.shard_map(
        body,
        mesh=mesh,
        in_specs=(act, ker, ker, act),
        out_specs=(act, act, ker, ker),
        check_vma=False,
    )
```

```python
import functools
import math

import jax
import jax.numpy as jnp
from jax import lax
from jax.experimental import pallas as pl
from jax.experimental.pallas import tpu as pltpu
from jax.sharding import PartitionSpec as P


LANES = 256
ROWS = 16


def shifted(values, dy, dx, side):
    plane = values.shape[1]
    amount = (-(dy * side + dx)) % plane
    if amount == 0:
        return values
    cell = lax.broadcasted_iota(jnp.int32, values.shape, 1)
    row, col = cell // side + dy, cell % side + dx
    inside = (row >= 0) & (row < side) & (col >= 0) & (col < side)
    return jnp.where(inside, pltpu.roll(values, amount, 1), 0.0)


def offsets(sign):
    return [(sign * (b - 1), sign * (c - 1)) for b in range(3) for c in range(3)]


def other_tap(sign):
    s = lax.axis_index("spatial")
    return 2 - 2 * s if sign > 0 else 2 * s


def product_over_channels(sign, side, own_ref, oth_ref, w_ref, y_ref, finish):
    held = w_ref.shape[0] // 27
    plane = own_ref.shape[1]
    third = 9 * held
    away = pl.multiple_of(other_tap(sign) * third, third)

    @pl.loop(0, plane // LANES)
    def _(n):
        cols = pl.ds(pl.multiple_of(n * LANES, LANES), LANES)
        y_ref[:, cols] = jnp.dot(
            w_ref[third : 2 * third, :], own_ref[:, cols], preferred_element_type=jnp.float32
        ) + jnp.dot(
            w_ref[pl.ds(away, third), :], oth_ref[:, cols], preferred_element_type=jnp.float32
        )

    @pl.loop(0, held // ROWS)
    def _(k):
        base = pl.multiple_of(k * ROWS, ROWS)
        total = None
        for t, (dy, dx) in enumerate(offsets(sign)):
            part = shifted(y_ref[pl.ds(base + t * held, ROWS), :], dy, dx, side)
            total = part if total is None else total + part
        finish(pl.ds(base, ROWS), total)


def forward_kernel(side, own_ref, oth_ref, w_ref, pre_ref, hid_ref, y_ref):
    def finish(rows, total):
        pre_ref[rows, :] = total
        hid_ref[rows, :] = (total / (1.0 + jnp.exp(-total))).astype(jnp.bfloat16)

    product_over_channels(1, side, own_ref, oth_ref, w_ref, y_ref, finish)


def backward_kernel(side, own_ref, oth_ref, w_ref, pre_ref, act_ref, y_ref):
    def finish(rows, total):
        pre = pre_ref[rows, :]
        sig = 1.0 / (1.0 + jnp.exp(-pre))
        act_ref[rows, :] = (total * sig * (1.0 + pre * (1.0 - sig))).astype(jnp.bfloat16)

    product_over_channels(-1, side, own_ref, oth_ref, w_ref, y_ref, finish)


NT = (((1,), (1,)), ((), ()))
TN = (((0,), (0,)), ((), ()))


def weight_kernel(sign, side, own_ref, oth_ref, far_own_ref, far_oth_ref, w_ref, grad_ref, out_ref, cols_ref):
    held = own_ref.shape[0]
    third = 9 * held
    half = third // 2

    @pl.loop(0, held // ROWS)
    def _(k):
        base = pl.multiple_of(k * ROWS, ROWS)
        for j, ref in enumerate((own_ref, oth_ref)):
            values = ref[pl.ds(base, ROWS), :].astype(jnp.float32)
            for t, (dy, dx) in enumerate(offsets(sign)):
                cols_ref[pl.ds(base + (j * 9 + t) * held, ROWS), :] = shifted(values, dy, dx, side).astype(jnp.bfloat16)

    mine = pl.multiple_of(lax.axis_index("spatial") * half, half)
    away = pl.multiple_of(other_tap(sign) * third, third)

    @pl.loop(0, far_own_ref.shape[0] // LANES)
    def _(n):
        rows = pl.ds(pl.multiple_of(n * LANES, LANES), LANES)
        far_own, far_oth = far_own_ref[rows, :], far_oth_ref[rows, :]
        grad_ref[:third, rows] = lax.dot_general(
            cols_ref[third:, :], far_own, NT, preferred_element_type=jnp.float32
        ).astype(jnp.bfloat16)
        grad_ref[third:, rows] = (
            lax.dot_general(cols_ref[pl.ds(mine, half), :], far_own, NT, preferred_element_type=jnp.float32)
            + lax.dot_general(cols_ref[pl.ds(third + mine, half), :], far_oth, NT, preferred_element_type=jnp.float32)
        ).astype(jnp.bfloat16)
        out_ref[rows, :] = (
            lax.dot_general(w_ref[third : 2 * third, rows], cols_ref[:third, :], TN, preferred_element_type=jnp.float32)
            + lax.dot_general(w_ref[pl.ds(away, third), rows], cols_ref[third:, :], TN, preferred_element_type=jnp.float32)
        ).astype(jnp.bfloat16)


def call(kernel, outs, scratch, flops, moved, *args):
    vmem = pl.BlockSpec(memory_space=pltpu.VMEM)
    return pl.pallas_call(
        kernel,
        out_shape=outs,
        in_specs=[vmem] * len(args),
        out_specs=jax.tree.map(lambda _: vmem, outs),
        scratch_shapes=scratch,
        cost_estimate=pl.CostEstimate(flops=flops, bytes_accessed=moved, transcendentals=0),
        compiler_params=pltpu.CompilerParams(vmem_limit_bytes=32 * 1024 * 1024),
    )(*args)


def swap(values):
    return lax.ppermute(values, "spatial", [(0, 1), (1, 0)])


def shift(values, axis, by):
    n = lax.axis_size(axis)
    return lax.ppermute(values, axis, [(i, (i + by) % n) for i in range(n)])


def gathered(values):
    n, rows = lax.axis_size("channel"), values.shape[0]
    if n > 4:
        return lax.all_gather(values, "channel", axis=0, tiled=True)
    me = lax.axis_index("channel")
    whole = jnp.zeros((n * rows,) + values.shape[1:], values.dtype)
    for k in range(n):
        piece = values if k == 0 else shift(values, "channel", k)
        whole = lax.dynamic_update_slice(whole, piece, (((me - k) % n) * rows, 0))
    return whole


def scattered(values):
    n = lax.axis_size("channel")
    if n > 4:
        return lax.psum_scatter(values, "channel", scatter_dimension=0, tiled=True)
    me, rows = lax.axis_index("channel"), values.shape[0] // n
    total = 0.0
    for k in range(n):
        piece = lax.dynamic_slice(values, (((me + k) % n) * rows, 0), (rows, values.shape[1]))
        piece = piece if k == 0 else shift(piece, "channel", k)
        total = total + piece.astype(jnp.float32)
    return total.astype(values.dtype)


def halved_and_joined(values, bits):
    n, me = lax.axis_size("samples"), lax.axis_index("samples")
    trade = lambda v, bit: lax.ppermute(v, "samples", [(i, i ^ bit) for i in range(n)])
    rows = values.shape[0]
    for bit in bits:
        high = (me // bit) % 2
        cols = values.shape[1] // 2
        cut = lambda at: lax.dynamic_slice(values, (0, at * cols), (rows, cols))
        kept, sent = cut(high), cut(1 - high)
        got = trade(sent, bit)
        values = (kept.astype(jnp.float32) + got.astype(jnp.float32)).astype(values.dtype)
    for bit in bits[::-1]:
        high = (me // bit) % 2
        got = trade(values, bit)
        values = jnp.concatenate([jnp.where(high == 0, values, got), jnp.where(high == 0, got, values)], axis=1)
    return values


def total_over_samples(part):
    if lax.axis_size("samples") != 4 or part.shape[1] % 512 or part.shape[0] % 16:
        return lax.psum(part, "samples")
    middle = part.shape[0] // 2
    return jnp.concatenate([halved_and_joined(part[:middle], (1, 2)), halved_and_joined(part[middle:], (2, 1))], axis=0)


def join_kernel(sign, mine_ref, theirs_ref, out_ref):
    block = pl.program_id(0)
    half = out_ref.shape[0]
    s = lax.axis_index("spatial")
    low = 1 if sign > 0 else 0
    source = jnp.where(block < 2, low, jnp.where(block > 3, 1 - low, block - 2))
    part = jnp.where(block < 2, block, jnp.where(block > 3, block - 4, 2))
    rows = pl.ds(pl.multiple_of(part * half, half), half)

    @pl.when(source == s)
    def _():
        out_ref[...] = mine_ref[rows, :].astype(jnp.float32)

    @pl.when(source != s)
    def _():
        out_ref[...] = theirs_ref[rows, :].astype(jnp.float32)


def joined(mine, theirs, sign, held):
    half, full = 9 * held // 2, mine.shape[1]
    whole = pl.BlockSpec(memory_space=pltpu.VMEM)
    out = pl.pallas_call(
        functools.partial(join_kernel, sign),
        out_shape=jax.ShapeDtypeStruct((6 * half, full), jnp.float32),
        grid=(6,),
        in_specs=[whole, whole],
        out_specs=pl.BlockSpec((half, full), lambda j: (j, 0)),
        cost_estimate=pl.CostEstimate(flops=0, bytes_accessed=36 * half * full, transcendentals=0),
        compiler_params=pltpu.CompilerParams(vmem_limit_bytes=16 * 1024 * 1024),
    )(mine, theirs)
    return out.reshape(27, held, full)


def body(features, conv_one, conv_two, cotangent):
    held, plane = features.shape[0], features.shape[3]
    full = conv_one.shape[2]
    side = math.isqrt(plane)
    third = 9 * held
    f32, b16 = jnp.float32, jnp.bfloat16
    flat = lambda v: v.reshape(held, plane)
    w_one, w_two = conv_one.reshape(27 * held, full), conv_two.reshape(27 * held, full)
    work = 2 * 2 * third * full * plane
    small = 6 * held * full

    x = gathered(flat(features))
    c = gathered(flat(cotangent))
    x_oth, c_oth = swap(x), swap(c)
    y_scratch = [pltpu.VMEM((third, plane), f32)]
    pre, hid = call(
        functools.partial(forward_kernel, side),
        (jax.ShapeDtypeStruct((held, plane), f32), jax.ShapeDtypeStruct((held, plane), b16)),
        y_scratch, work, small, x, x_oth, w_one,
    )
    hid_oth = swap(hid)
    act = call(
        functools.partial(backward_kernel, side),
        jax.ShapeDtypeStruct((held, plane), b16),
        y_scratch, work, small, c, c_oth, w_two, pre,
    )
    act_oth = swap(act)
    weights = lambda sign, own, oth, far, far_oth, w: call(
        functools.partial(weight_kernel, sign, side),
        (jax.ShapeDtypeStruct((third + third // 2, full), b16), jax.ShapeDtypeStruct((full, plane), b16)),
        [pltpu.VMEM((2 * third, plane), b16)], 2 * work, small, own, oth, far, far_oth, w,
    )
    part_two, mix_two = weights(1, hid, hid_oth, c, c_oth, w_two)
    part_one, mix_one = weights(-1, act, act_oth, x, x_oth, w_one)
    mixed = scattered(mix_two).reshape(features.shape)
    input_grad = scattered(mix_one).reshape(features.shape)
    sum_two = total_over_samples(part_two)
    sum_one = total_over_samples(part_one)
    grad_two = joined(sum_two, swap(sum_two), 1, held)
    grad_one = joined(sum_one, swap(sum_one), -1, held)
    return mixed, input_grad, grad_one, grad_two


def solution(mesh):
    act = P("channel", "samples", "spatial", None)
    ker = P(None, "channel", None)
    return jax.shard_map(
        body,
        mesh=mesh,
        in_specs=(act, ker, ker, act),
        out_specs=(act, act, ker, ker),
        check_vma=False,
    )
```
